256 devices in a mesh: wide: 32 (over x, y, core), narrow: 8 (over z).
Axes of the slice: x: 4, y: 4, z: 8, core: 2. Of those that a mesh axis runs over, the one named last changes fastest.
Arguments:
- residual: bfloat16 [8192, 4608], P('wide'), may hold values from -6 to 6
- pre_gain: bfloat16 [4608], replicated, may hold values from 0.5 to 1.5
- query_weight: bfloat16 [4608, 4096], P('wide', 'narrow'), may hold values from -0.09375 to 0.09375
- key_weight: bfloat16 [4608, 2048], P('wide', 'narrow'), may hold values from -0.09375 to 0.09375
- value_weight: bfloat16 [4608, 2048], P('wide', 'narrow'), may hold values from -0.09375 to 0.09375
- output_weight: bfloat16 [4096, 4608], P('narrow', 'wide'), may hold values from -1 to 1
- adapter_down: bfloat16 [4608, 768], P('wide', 'narrow'), may hold values from -0.09375 to 0.09375
- adapter_up_query: bfloat16 [256, 4096], P(None, 'narrow'), may hold values from -1.5 to 1.5
- adapter_up_key: bfloat16 [256, 2048], P(None, 'narrow'), may hold values from -1.5 to 1.5
- adapter_up_value: bfloat16 [256, 2048], P(None, 'narrow'), may hold values from -1.5 to 1.5
- adapter_down_out: bfloat16 [4096, 256], P('narrow'), may hold values from -0.09375 to 0.09375
- adapter_up_out: bfloat16 [256, 4608], P(None, 'narrow'), may hold values from -1.5 to 1.5
- post_gain: bfloat16 [4608], P('narrow'), may hold values from 0.5 to 1.5
- sink_logits: float32 [32], P('narrow'), may hold values from -1 to 130
- prompt_lengths: int32 [4], replicated, may hold values from 1 to 4096, 8192 in all
- prompt_adapters: int32 [4], replicated, may hold values from 0 to 15
Outputs:
- layer_out: bfloat16 [8192, 4608], P('wide', 'narrow')
The draws below stay inside these ranges and needn't reach their ends.
All inputs are finite; a program needn't handle non-finite values.
Results may differ from the reference program's by a relative error of at most 0.022.
Values may be sent and summed in bfloat16 or wider, within the bound.
A program may use at most 128 MiB of HBM per device.

```python
import math
import jax
import jax.numpy as jnp
import numpy as np
from jax import lax

D = 4608
HEADS = 32
KV_HEADS = 16
HEAD_DIM = 128
RANK = 16
ADAPTERS = 16
PROMPTS = 4
TOKENS = 8192


def draw_output_weight(key, part):
    rows = HEADS * HEAD_DIM
    column = jnp.arange(D, dtype=jnp.float32) / (D - 1)
    base = jnp.clip(jax.random.normal(key, (rows, D), jnp.float32), -6.0, 6.0)
    scale = 1.0 + column
    return (base * scale[None, :] / math.sqrt(rows)).astype(jnp.bfloat16)


def draw_sink_logits(key, part):
    values = jax.random.uniform(key, (HEADS,), jnp.float32, -1.0, 3.0)
    return values


def plant(values, rng, low, largest):
    index_at = [jax.random.randint(jax.random.fold_in(rng, axis), (), 0, length) for axis, length in enumerate(values.shape)]
    longest = values.shape.index(max(values.shape))
    neighbour = index_at[:longest] + [(index_at[longest] + 1) % values.shape[longest]] + index_at[longest + 1:]
    return values.at[tuple(index_at)].set(low).at[tuple(neighbour)].set(largest)


def block_levels(stream_key, extent, cuts, least, top_value):
    def one(axis_at, blocks):
        heights = jax.random.uniform(jax.random.fold_in(jax.random.fold_in(stream_key, 6), axis_at), (blocks,), jnp.float32, least / len(cuts), top_value / len(cuts))
        return jnp.repeat(jnp.exp(heights), extent[axis_at] // blocks).reshape((-1,) + (1,) * (len(extent) - axis_at - 1))

    gain = one(*cuts[0])
    for cut in cuts[1:]:
        gain = gain * one(*cut)
    return gain


def length_profile(count, total, most, slope):
    loads = [(1 << 20) // math.isqrt(rank ** slope) + 1 for rank in range(2, count + 1)]
    rest, counts = total - most - (count - 1), [1] * (count - 1)
    while rest > 0:
        movable = [i for i in range(count - 1) if counts[i] < most]
        whole, budget = sum([loads[i] for i in movable]), rest
        for i in movable:
            more = min(most - counts[i], max(1, budget * loads[i] // whole), rest)
            counts[i] = counts[i] + more
            rest = rest - more
    return np.array([most] + counts)


def ragged_sizes(rng, count, total, limit, slope):
    if count == 2:
        one = jax.random.randint(rng, (), max(1, total - limit), min(limit, total - 1) + 1)
        return jnp.stack([one, total - one])
    sizes = jnp.asarray(length_profile(count, total, limit, slope), jnp.int32)
    couples = (count - 1) // 2
    giver, receiver = sizes[1:1 + 2 * couples:2], sizes[2:2 + 2 * couples:2]
    margin = jnp.minimum(giver - 1, limit - receiver)
    passed = jax.random.randint(jax.random.fold_in(rng, 1), (couples,), 0, 1 << 20) % (margin + 1)
    sizes = sizes.at[1:1 + 2 * couples:2].set(giver - passed).at[2:2 + 2 * couples:2].set(receiver + passed)
    return sizes[jax.random.permutation(jax.random.fold_in(rng, 2), count)]


def bell_draw(stream_key, shape, spread, limit, pieces=(), held_as=jnp.bfloat16):
    factor_of = block_levels(stream_key, shape, pieces, -0.22, 0.18) if pieces else 1.0
    entries = jax.random.normal(stream_key, shape, jnp.float32) * spread * factor_of
    return jnp.minimum(jnp.maximum(entries, -limit), limit).astype(held_as)


def setup_inputs(seed: int = 0) -> dict:
    seeds = jax.random.split(jax.random.key(seed), 17)
    return {
        "residual": bell_draw(seeds[0], (TOKENS, D), 1.0, 6.0, ((0, 32),)),
        "pre_gain": jnp.clip(1.0 + 0.1 * jax.random.normal(seeds[1], (D,), jnp.float32), 0.5, 1.5).astype(jnp.bfloat16),
        "query_weight": bell_draw(seeds[2], (D, HEADS * HEAD_DIM), D ** -0.5, 0.09375, ((0, 32), (1, 8))),
        "key_weight": bell_draw(seeds[3], (D, KV_HEADS * HEAD_DIM), D ** -0.5, 0.09375, ((0, 32), (1, 8))),
        "value_weight": bell_draw(seeds[4], (D, KV_HEADS * HEAD_DIM), D ** -0.5, 0.09375, ((0, 32), (1, 8))),
        "output_weight": draw_output_weight(jax.random.fold_in(seeds[16], 71), 0),
        "adapter_down": bell_draw(seeds[6], (D, 3 * ADAPTERS * RANK), D ** -0.5, 0.09375, ((0, 32), (1, 8))),
        "adapter_up_query": bell_draw(seeds[7], (ADAPTERS * RANK, HEADS * HEAD_DIM), RANK ** -0.5, 1.5, ((1, 8),)),
        "adapter_up_key": bell_draw(seeds[8], (ADAPTERS * RANK, KV_HEADS * HEAD_DIM), RANK ** -0.5, 1.5, ((1, 8),)),
        "adapter_up_value": bell_draw(seeds[9], (ADAPTERS * RANK, KV_HEADS * HEAD_DIM), RANK ** -0.5, 1.5, ((1, 8),)),
        "adapter_down_out": bell_draw(seeds[10], (HEADS * HEAD_DIM, ADAPTERS * RANK), (HEADS * HEAD_DIM) ** -0.5, 0.09375, ((0, 8),)),
        "adapter_up_out": bell_draw(seeds[11], (ADAPTERS * RANK, D), RANK ** -0.5, 1.5, ((1, 8),)),
        "post_gain": jnp.clip(1.0 + 0.1 * jax.random.normal(seeds[12], (D,), jnp.float32), 0.5, 1.5).astype(jnp.bfloat16),
        "sink_logits": draw_sink_logits(jax.random.fold_in(seeds[16], 71), 0),
        "prompt_lengths": ragged_sizes(seeds[14], PROMPTS, TOKENS, TOKENS // 2, 2).astype(jnp.int32),
        "prompt_adapters": plant(jax.random.randint(seeds[15], (PROMPTS,), 0, ADAPTERS), jax.random.fold_in(seeds[15], 1), 0, ADAPTERS - 1).astype(jnp.int32),
    }


epsilon = 1e-06
adapter_scale = 0.5
rotary_base = 10000.0
score_scale = 1.0 / 12.0

def token_layout(prompt_lengths, count, first):
    ends = jnp.cumsum(prompt_lengths, dtype=jnp.int32)
    starts = (ends - prompt_lengths).astype(jnp.int32)
    places = first + jnp.arange(count, dtype=jnp.int32)
    member = jnp.logical_and(places[:, None] >= starts[None, :], places[:, None] < ends[None, :]).astype(jnp.int32)
    labels = jnp.arange(prompt_lengths.shape[0], dtype=jnp.int32)
    prompt = lax.optimization_barrier(jnp.sum(member * labels[None, :], axis=1)).astype(jnp.int32)
    position = (places - lax.optimization_barrier(jnp.sum(member * starts[None, :], axis=1))).astype(jnp.int32)
    return (member, prompt, position)

def norm_factor(values):
    return lax.rsqrt(lax.optimization_barrier(jnp.mean(values * values, axis=-1, keepdims=True)) + epsilon)

def rotate(values, position):
    half = values.shape[-1] // 2
    exponent = jnp.arange(half, dtype=jnp.float32) * (2.0 / values.shape[-1])
    frequency = jnp.power(jnp.float32(rotary_base), -exponent)
    angle = position.astype(jnp.float32)[:, None] * frequency[None, :]
    cosine = jnp.cos(angle)[:, None, :]
    sine = jnp.sin(angle)[:, None, :]
    first_half = values[..., :half]
    second_half = values[..., half:]
    return jnp.concatenate([first_half * cosine - second_half * sine, second_half * cosine + first_half * sine], axis=-1)

def select_codes(codes, adapter, projections, adapters):
    count = codes.shape[0]
    width = codes.shape[1] // (adapters * projections)
    shaped = codes.reshape(count, adapters, projections, width)
    onehot = (adapter[:, None] == jnp.arange(adapters, dtype=jnp.int32)[None, :]).astype(codes.dtype)
    kept = shaped * onehot[:, :, None, None]
    return [kept[:, :, slot, :].reshape(count, adapters * width) for slot in range(projections)]

def reference(residual, pre_gain, query_weight, key_weight, value_weight, output_weight, adapter_down, adapter_up_query, adapter_up_key, adapter_up_value, adapter_down_out, adapter_up_out, post_gain, sink_logits, prompt_lengths, prompt_adapters):
    member, prompt, position = token_layout(prompt_lengths, TOKENS, jnp.int32(0))
    adapter = lax.optimization_barrier(jnp.sum(member * prompt_adapters[None, :], axis=1)).astype(jnp.int32)
    stream = residual.astype(jnp.float32)
    normed = (stream * norm_factor(stream) * pre_gain.astype(jnp.float32)[None, :]).astype(jnp.bfloat16)
    codes = jnp.dot(normed, adapter_down, preferred_element_type=jnp.float32).astype(jnp.bfloat16)
    chosen = select_codes(codes, adapter, 3, ADAPTERS)
    query = jnp.dot(normed, query_weight, preferred_element_type=jnp.float32) + adapter_scale * jnp.dot(chosen[0], adapter_up_query, preferred_element_type=jnp.float32)
    key = jnp.dot(normed, key_weight, preferred_element_type=jnp.float32) + adapter_scale * jnp.dot(chosen[1], adapter_up_key, preferred_element_type=jnp.float32)
    value = jnp.dot(normed, value_weight, preferred_element_type=jnp.float32) + adapter_scale * jnp.dot(chosen[2], adapter_up_value, preferred_element_type=jnp.float32)
    query = rotate(query.reshape(TOKENS, HEADS, HEAD_DIM), position).astype(jnp.bfloat16)
    keys = rotate(key.reshape(TOKENS, KV_HEADS, HEAD_DIM), position).astype(jnp.bfloat16)
    values = value.astype(jnp.bfloat16).reshape(TOKENS, KV_HEADS, HEAD_DIM)
    group = HEADS // KV_HEADS
    places = jnp.arange(TOKENS, dtype=jnp.int32)
    block = math.gcd(TOKENS, 1024)

    def one_head(head):
        head_query = lax.dynamic_index_in_dim(query, head, 1, keepdims=False)
        head_key = lax.dynamic_index_in_dim(keys, (head // group).astype(jnp.int32), 1, keepdims=False)
        head_value = lax.dynamic_index_in_dim(values, (head // group).astype(jnp.int32), 1, keepdims=False)
        sink = lax.dynamic_index_in_dim(sink_logits.astype(jnp.float32), head, 0, keepdims=False)

        def one_block(start):
            rows = lax.dynamic_slice_in_dim(head_query, start, block, 0)
            row_prompt = lax.dynamic_slice_in_dim(prompt, start, block, 0)
            row_place = lax.dynamic_slice_in_dim(places, start, block, 0)
            scores = jnp.dot(rows, head_key.T, preferred_element_type=jnp.float32) * score_scale
            allowed = jnp.logical_and(row_prompt[:, None] == prompt[None, :], row_place[:, None] >= places[None, :])
            scores = jnp.where(allowed, scores, -1e+30)
            top = jnp.maximum(lax.optimization_barrier(jnp.max(scores, axis=1)), sink)
            weights = jnp.where(allowed, jnp.exp(scores - top[:, None]), 0.0)
            total = lax.optimization_barrier(jnp.sum(weights, axis=1)) + jnp.exp(sink - top)
            mixed = jnp.dot(weights.astype(jnp.bfloat16), head_value, preferred_element_type=jnp.float32)
            return mixed / total[:, None]
        starts = jnp.arange(TOKENS // block, dtype=jnp.int32) * block
        return lax.map(one_block, starts).reshape(TOKENS, HEAD_DIM)
    heads_out = lax.map(one_head, jnp.arange(HEADS, dtype=jnp.int32))
    attended = jnp.transpose(heads_out, (1, 0, 2)).reshape(TOKENS, HEADS * HEAD_DIM).astype(jnp.bfloat16)
    codes_out = jnp.dot(attended, adapter_down_out, preferred_element_type=jnp.float32).astype(jnp.bfloat16)
    chosen_out = select_codes(codes_out, adapter, 1, ADAPTERS)[0]
    projected = jnp.dot(attended, output_weight, preferred_element_type=jnp.float32) + adapter_scale * jnp.dot(chosen_out, adapter_up_out, preferred_element_type=jnp.float32)
    mixed = stream + projected * norm_factor(projected) * post_gain.astype(jnp.float32)[None, :]
    return mixed.astype(jnp.bfloat16)
```

```python
import functools

import jax
import jax.numpy as jnp
import numpy as np
from jax import lax
from jax.experimental import pallas as pl
from jax.experimental.pallas import tpu as pltpu
from jax.sharding import PartitionSpec as P

MESH = pl.DeviceIdType.MESH
HEAD = 128
ADAPTERS = 16
RANK = 16
D = 4608
SIDE = 4
CHIPS = 16
PLANES = 8
ROWS = D // (2 * CHIPS)
EPS = 1e-06
SCALE = 0.5
SCORE = 1.0 / 12.0
F32 = jnp.float32
BF16 = jnp.bfloat16


def dot(a, b, ca, cb):
    return lax.dot_general(a, b, (((ca,), (cb,)), ((), ())), preferred_element_type=F32)


class Place:
    def __init__(self):
        wide = lax.axis_index("wide")
        self.plane = lax.axis_index("narrow")
        self.core = lax.rem(wide, 2)
        self.chip = wide // 2
        self.x = self.chip // SIDE
        self.y = lax.rem(self.chip, SIDE)
        self.wide = wide

    def chip_at(self, dx, dy):
        return lax.rem(self.x + dx, SIDE) * SIDE + lax.rem(self.y + dy, SIDE)

    def dev(self, dx, dy, core):
        return (self.chip_at(dx, dy) * 2 + core, self.plane)

    def other_plane(self, dz, core=None):
        core = self.core if core is None else core
        return (self.chip * 2 + core, lax.rem(self.plane + dz, PLANES))


def enter(peers):
    barrier = pltpu.get_barrier_semaphore()
    for peer in peers:
        pl.semaphore_signal(barrier, inc=1, device_id=peer, device_id_type=MESH)
    pl.semaphore_wait(barrier, len(peers))


def plane_peers(me):
    peers = [me.dev(0, 0, 1 - me.core)]
    for dx, dy in ((1, 0), (3, 0), (0, 1), (0, 3)):
        peers += [me.dev(dx, dy, 0), me.dev(dx, dy, 1)]
    return peers


def landed(ref, sem):
    pltpu.make_async_copy(ref, ref, sem).wait()


class Part:
    def __init__(self, me, order, unit, send, recv):
        self.me, self.order, self.unit, self.send, self.recv = me, order, unit, send, recv
        self.sent = []

    def rel(self, f, g):
        return (f, g) if self.order == "xy" else (g, f)

    def at(self, f, g):
        return self.unit(self.me.chip_at(*self.rel(f, g)))

    def target(self, f, g, core):
        return self.me.dev(*self.rel(f, g), core)

    def push(self, src, dst, sem, device):
        copy = pltpu.make_async_remote_copy(
            src_ref=src,
            dst_ref=dst,
            send_sem=self.send.at[len(self.sent)],
            recv_sem=sem,
            device_id=device,
            device_id_type=MESH,
        )
        copy.start()
        self.sent.append(copy)

    def label(self, f, g):
        return self.recv.at[f * 4 + g]

    def single(self, f, s):
        return self.recv.at[16 + f * 2 + s]

    def start_pairs(self, pieces):
        me = self.me
        mine = self.unit(me.chip)
        for d in (1, 3):
            for core in (me.core, 1 - me.core):
                for src, sub in pieces(core):
                    self.push(src, sub(mine, me.core), self.single(4 - d, me.core), self.target(d, 0, core))
        for src, sub in pieces(1 - me.core):
            self.push(src, sub(mine, me.core), self.single(0, me.core), self.target(0, 0, 1 - me.core))
        for n, (src, sub) in enumerate(pieces(me.core)):
            pltpu.make_async_copy(src, sub(mine, me.core), self.single(0, me.core)).start()

    def start_own(self, src, dst):
        self.own = src
        for d in (1, 3):
            self.push(src, dst, self.label(4 - d, 0), self.target(d, 0, self.me.core))

    def far(self):
        return 3 - 2 * self.me.core, 1 + 2 * self.me.core

    def spread(self, f, src=None):
        unit = self.at(f, 0)
        for d in (1, 3):
            self.push(unit if src is None else src, unit, self.label(f, 4 - d), self.target(0, d, self.me.core))

    def second_pairs(self):
        landed(self.at(0, 0).at[0], self.single(0, 0))
        landed(self.at(0, 0).at[1], self.single(0, 1))
        self.spread(0)
        for f in (1, 3):
            for s in (0, 1):
                landed(self.at(f, 0).at[s], self.single(f, s))
        self.after_first()

    def second_own(self):
        self.spread(0, self.own)
        for f in (1, 3):
            landed(self.at(f, 0), self.label(f, 0))
        self.after_first()

    def after_first(self):
        source, step = self.far()
        unit = self.at(source, 0)
        self.push(unit, unit, self.label(2, 0), self.target(step, 0, self.me.core))
        for f in (1, 3):
            self.spread(f)

    def third(self):
        landed(self.at(2, 0), self.label(2, 0))
        self.spread(2)

    def fourth(self, fs=(0, 1, 3, 2)):
        source, step = self.far()
        for f in fs:
            for g in (1, 3):
                landed(self.at(f, g), self.label(f, g))
            unit = self.at(f, source)
            self.push(unit, unit, self.label(f, 2), self.target(0, step, self.me.core))

    def last(self, f):
        landed(self.at(f, 2), self.label(f, 2))

    def finish(self):
        for copy in self.sent:
            copy.wait_send()


def token_facts(lengths, places, adapters=None):
    start = jnp.zeros_like(places)
    adapter = jnp.zeros_like(places)
    begin = jnp.int32(0)
    for p in range(4):
        end = begin + lengths[p]
        member = jnp.logical_and(places >= begin, places < end)
        start = jnp.where(member, begin, start)
        if adapters is not None:
            adapter = jnp.where(member, adapters[p], adapter)
        begin = end
    return start, adapter


def choose(codes, adapter):
    tokens = codes.shape[1]
    spread = jnp.broadcast_to(codes[None], (ADAPTERS, RANK, tokens)).reshape(ADAPTERS * RANK, tokens)
    row = lax.broadcasted_iota(jnp.int32, (ADAPTERS * RANK, tokens), 0) // RANK
    return jnp.where(row == adapter, spread, 0.0).astype(BF16)


def project_kernel(
    lengths, adapters, residual, gain, qw, kw, vw, dn, upq, upk, upv, freq,
    q_out, k_out, v_out,
    other, normed, wq, wkv, down, qacc, kvacc, mixed, mixed_in, code_send, codes,
    send, recv, csend, crecv, rsem,
):
    me = Place()
    c = me.core
    half = residual.shape[0]
    down[...] = jnp.zeros_like(down)
    zpeers = []
    for dz in range(1, PLANES):
        zpeers += [me.other_plane(dz, 0), me.other_plane(dz, 1)]
    enter(plane_peers(me) + zpeers)

    dpart = Part(me, "xy", lambda j: down.at[j, c], send.at[0], recv.at[0])
    qpart = Part(me, "xy", lambda j: wq.at[j], send.at[1], recv.at[1])
    kvpart = Part(me, "yx", lambda j: wkv.at[j], send.at[2], recv.at[2])

    def q_pieces(core):
        cols = pl.ds(pl.multiple_of(core * 256, 256), 256)
        return [(qw.at[:, cols], lambda unit, s: unit.at[s])]

    def kv_pieces(core):
        cols = pl.ds(pl.multiple_of(core * 128, 128), 128)
        return [
            (kw.at[:, cols], lambda unit, s: unit.at[s, :, pl.ds(0, 128)]),
            (vw.at[:, cols], lambda unit, s: unit.at[s, :, pl.ds(128, 128)]),
        ]

    dpart.start_own(dn, down.at[me.chip, c])
    own_down = pltpu.make_async_copy(dn, down.at[me.chip, c], rsem.at[2])
    own_down.start()
    swap = pltpu.make_async_remote_copy(
        src_ref=residual, dst_ref=other, send_sem=rsem.at[0], recv_sem=rsem.at[1],
        device_id=me.dev(0, 0, 1 - c), device_id_type=MESH,
    )
    swap.start()
    qpart.start_pairs(q_pieces)
    kvpart.start_pairs(kv_pieces)

    def norm(source, first):
        def body(i, carry):
            rows = pl.ds(pl.multiple_of(i * 32, 32), 32)
            values = source[rows, :].astype(F32)
            factor = lax.rsqrt(jnp.mean(values * values, axis=1, keepdims=True) + EPS)
            target = pl.ds(pl.multiple_of(first + i * 32, 32), 32)
            normed[target, :] = (values * factor * gain[...].astype(F32)).astype(BF16)
            return carry

        lax.fori_loop(0, half // 32, body, 0)

    norm(residual, c * half)
    dpart.second_own()
    qpart.second_pairs()
    kvpart.second_pairs()
    swap.wait_recv()
    norm(other, (1 - c) * half)
    dpart.third()
    qpart.third()
    kvpart.third()
    dpart.fourth()
    for f in (0, 1, 3, 2):
        dpart.last(f)
    own_down.wait()

    first = me.chip * (2 * half)
    lanes = first + lax.broadcasted_iota(jnp.int32, (1, 2 * half), 1)
    unused, adapter = token_facts(lengths, lanes, adapters)
    part = dot(normed[...], down[...].reshape(D, 128), 1, 0).T
    kept = jnp.where(adapter == 2 * me.plane, part[0:48], 0.0) + jnp.where(
        adapter == 2 * me.plane + 1, part[48:96], 0.0
    )
    mixed[0] = kept[:, :half]
    mixed[1] = kept[:, half:]
    qpart.fourth()
    kvpart.fourth()
    trade = pltpu.make_async_remote_copy(
        src_ref=mixed.at[1 - c], dst_ref=mixed_in, send_sem=rsem.at[3], recv_sem=rsem.at[4],
        device_id=me.dev(0, 0, 1 - c), device_id_type=MESH,
    )
    trade.start()

    places = first + lax.broadcasted_iota(jnp.int32, (2 * half, HEAD), 0)
    start, unused = token_facts(lengths, places)
    angle = (places - start).astype(F32) * freq[...]
    cosine = jnp.cos(angle)
    sine = jnp.sin(angle)
    low = lax.broadcasted_iota(jnp.int32, (2 * half, HEAD), 1) < HEAD // 2
    sine = jnp.where(low, -sine, sine)

    trade.wait_recv()
    total = (mixed[c] + mixed_in[...]).astype(BF16)
    code_send[...] = total
    codes[me.plane, c] = total
    def chunk(buf, x):
        return buf[pl.ds(x * SIDE, SIDE)].reshape(D // SIDE, 256)

    def multiply(acc, buf, o, opening):
        x = lax.rem(me.x + o, SIDE)
        cols = pl.ds(pl.multiple_of(x * (D // SIDE), 128), D // SIDE)
        value = dot(normed[:, cols], chunk(buf, x), 1, 0)
        if opening:
            acc[...] = value
        else:
            acc[...] += value

    qpart.last(0)
    multiply(qacc, wq, 0, True)
    code_copies = []
    targets = [(0, 1 - c)] + [(dz, core) for dz in range(1, PLANES) for core in (c, 1 - c)]
    for n, (dz, core) in enumerate(targets):
        copy = pltpu.make_async_remote_copy(
            src_ref=code_send, dst_ref=codes.at[me.plane, c], send_sem=csend.at[n],
            recv_sem=crecv.at[me.plane, c], device_id=me.other_plane(dz, core), device_id_type=MESH,
        )
        copy.start()
        code_copies.append(copy)
    for f in (1, 3, 2):
        qpart.last(f)
        multiply(qacc, wq, f, False)
    for f in (0, 1, 3, 2):
        kvpart.last(f)
    for o in (0, 1, 3, 2):
        multiply(kvacc, wkv, o, o == 0)

    landed(codes.at[me.plane, 1 - c], crecv.at[me.plane, 1 - c])
    for dz in range(1, PLANES):
        z = lax.rem(me.plane + dz, PLANES)
        for core in (0, 1):
            landed(codes.at[z, core], crecv.at[z, core])
    whole = jnp.sum(codes[...].astype(F32), axis=0)
    whole = jnp.concatenate([whole[0], whole[1]], axis=1)

    def low_rank(slot, up, width):
        chosen = choose(whole[slot * RANK:(slot + 1) * RANK], adapter)
        cols = pl.ds(pl.multiple_of(c * width, width), width)
        return SCALE * dot(chosen, up[:, cols], 0, 0)

    def rotate(values):
        return values * cosine + pltpu.roll(values, HEAD // 2, 1) * sine

    query = qacc[...] + low_rank(0, upq, 256)
    q_out[:, :HEAD] = rotate(query[:, :HEAD]).astype(BF16)
    q_out[:, HEAD:] = rotate(query[:, HEAD:]).astype(BF16)
    k_out[...] = rotate(kvacc[:, :HEAD] + low_rank(1, upk, HEAD)).astype(BF16)
    v_out[...] = (kvacc[:, HEAD:] + low_rank(2, upv, HEAD)).astype(BF16)

    for copy in code_copies + [swap, trade]:
        copy.wait_send()
    for part in (dpart, qpart, kvpart):
        part.finish()


def attend_kernel(
    lengths, adapters, sinks, q, k, v, dn_out,
    att_out,
    kbuf, vbuf, top, total, acc,
    send, recv, own,
):
    me = Place()
    c = me.core
    tokens = q.shape[0]
    enter(plane_peers(me))
    kpart = Part(me, "xy", lambda j: kbuf.at[j], send.at[0], recv.at[0])
    vpart = Part(me, "yx", lambda j: vbuf.at[j], send.at[1], recv.at[1])
    kpart.start_own(k, kbuf.at[me.chip])
    vpart.start_own(v, vbuf.at[me.chip])

    first = me.chip * tokens
    places = first + lax.broadcasted_iota(jnp.int32, (1, tokens), 1)
    start, adapter = token_facts(lengths, places, adapters)
    for h in (0, 1):
        top[h] = jnp.full((1, tokens), sinks[2 * c + h], F32)
        total[h] = jnp.ones((1, tokens), F32)
        acc[h] = jnp.zeros((HEAD, tokens), F32)

    def block(key, value, chip):
        at = chip * tokens + lax.broadcasted_iota(jnp.int32, (tokens, tokens), 0)
        allowed = jnp.logical_and(at <= places, at >= start)
        for h in (0, 1):
            scores = dot(key, q[:, h * HEAD:(h + 1) * HEAD], 1, 1) * SCORE
            scores = jnp.where(allowed, scores, -1e30)
            old = top[h]
            fresh = jnp.maximum(old, jnp.max(scores, axis=0, keepdims=True))
            weights = jnp.exp(scores - fresh)
            factor = jnp.exp(old - fresh)
            total[h] = total[h] * factor + jnp.sum(weights, axis=0, keepdims=True)
            acc[h] = acc[h] * factor + dot(value, weights.astype(BF16), 0, 0)
            top[h] = fresh

    def visit(fx, fy):
        chip = me.chip_at(fx, fy)

        @pl.when(jnp.logical_and(chip < me.chip, chip + 8 >= me.chip))
        def _():
            block(kbuf[chip], vbuf[chip], chip)

    block(k[...], v[...], me.chip)
    kpart.second_own()
    vpart.second_own()
    kpart.third()
    vpart.third()
    kpart.fourth()
    vpart.fourth()

    def near(i, carry):
        a, b = i // 3, lax.rem(i, 3)
        visit(a + a // 2, b + b // 2)
        return carry

    lax.fori_loop(1, 9, near, 0)
    for f in (0, 1, 3, 2):
        kpart.last(f)
        vpart.last(f)

    def rest(i, carry):
        a = jnp.maximum(i - 4, 0)
        edge = i < 4
        visit(jnp.where(edge, 2, a + a // 2), jnp.where(edge, i, 2))
        return carry

    lax.fori_loop(0, 7, rest, 0)

    kpart.finish()
    vpart.finish()
    heads = jnp.concatenate([acc[0] / total[0], acc[1] / total[1]], axis=0).astype(BF16)
    att_out[0:2 * HEAD] = heads
    rows = pl.ds(pl.multiple_of(c * 256, 256), 256)
    terms = dot(dn_out[rows, :], heads, 0, 0)
    row = lax.broadcasted_iota(jnp.int32, terms.shape, 0) // RANK
    terms = jnp.where(row == adapter, terms, 0.0)
    terms = jnp.sum(terms.reshape(ADAPTERS, RANK, tokens), axis=0)
    att_out[2 * HEAD:2 * HEAD + RANK] = terms.astype(BF16)


def output_kernel(
    lengths, adapters, att, wo, up_out, post_gain, stream,
    out,
    ring, woa, wob, acc, swap_send, swap_in, square, squares,
    send, recv, zsend, zrecv, ssend, srecv, own,
):
    me = Place()
    c = me.core
    half = stream.shape[0]
    zpeers = [me.other_plane(dz) for dz in range(1, PLANES)]
    enter(plane_peers(me) + zpeers)

    subs = (pl.ds(0, 128), pl.ds(128, 144))
    zcopies = []

    def hop(src, slot, side, d, h):
        copy = pltpu.make_async_remote_copy(
            src_ref=src, dst_ref=ring.at[slot, subs[h]], send_sem=zsend.at[len(zcopies)],
            recv_sem=zrecv.at[side * 10 + d * 2 + h],
            device_id=me.other_plane(1 if side == 0 else PLANES - 1), device_id_type=MESH,
        )
        copy.start()
        zcopies.append(copy)

    def plane_of(side, d):
        return lax.rem(me.plane + (PLANES - d if side == 0 else d), PLANES)

    def arrive(side, d, h):
        landed(ring.at[plane_of(side, d), subs[h]], zrecv.at[side * 10 + d * 2 + h])

    for h in (0, 1):
        for side in (0, 1):
            hop(att.at[subs[h]], me.plane, side, 1, h)
    keep = pltpu.make_async_copy(att, ring.at[me.plane], own.at[0])
    keep.start()

    apart = Part(me, "xy", lambda j: woa.at[j], send.at[0], recv.at[0])
    bpart = Part(me, "yx", lambda j: wob.at[j], send.at[1], recv.at[1])

    def pieces(offset):
        def of(core):
            cols = pl.ds(pl.multiple_of(core * 256 + offset, 128), 128)
            return [(wo.at[:, cols], lambda unit, s: unit.at[s])]

        return of

    apart.start_pairs(pieces(0))
    bpart.start_pairs(pieces(128))

    def pass_on(d):
        for h in (0, 1):
            for side in (0, 1):
                arrive(side, d, h)
                if d < 3 or h == side:
                    slot = plane_of(side, d)
                    hop(ring.at[slot, subs[h]], slot, side, d + 1, h)

    def multiply(z, opening=False):
        weight = jnp.concatenate(
            [woa[pl.ds(2 * z, 2)].reshape(576, 128), wob[pl.ds(2 * z, 2)].reshape(576, 128)], axis=1
        )
        value = dot(weight, ring[z, pl.ds(0, 256)], 1, 0)
        if opening:
            acc[0:576] = value
        else:
            acc[0:576] += value

    apart.second_pairs()
    bpart.second_pairs()
    apart.third()
    bpart.third()
    pass_on(1)
    apart.fourth()
    bpart.fourth()
    pass_on(2)
    for f in (0, 1, 3, 2):
        apart.last(f)
        bpart.last(f)
    keep.wait()
    multiply(me.plane, True)
    for d in (1, 2):
        for side in (0, 1):
            multiply(plane_of(side, d))
    pass_on(3)
    for side in (0, 1):
        multiply(plane_of(side, 3))
    arrive(0, 4, 0)
    arrive(1, 4, 1)
    multiply(plane_of(0, 4))

    code_sum = jnp.sum(ring[:, pl.ds(256, RANK)].astype(F32), axis=0)
    theirs = pl.ds(pl.multiple_of((1 - c) * half, 256), half)
    mine = pl.ds(pl.multiple_of(c * half, 256), half)
    acc[576:592] = code_sum
    swap_send[...] = acc[:, theirs].astype(BF16)
    first = me.chip * (2 * half) + c * half
    places = first + lax.broadcasted_iota(jnp.int32, (1, half), 1)
    unused, adapter = token_facts(lengths, places, adapters)
    swap = pltpu.make_async_remote_copy(
        src_ref=swap_send, dst_ref=swap_in, send_sem=own.at[1], recv_sem=own.at[2],
        device_id=me.dev(0, 0, 1 - c), device_id_type=MESH,
    )
    swap.start()
    swap.wait_recv()
    merged = acc[:, mine] + swap_in[...].astype(F32)
    chosen = choose(merged[576:592].astype(BF16).astype(F32), adapter)
    projected = merged[0:576] + SCALE * dot(up_out[...], chosen, 0, 0)
    sums = jnp.sum(projected * projected, axis=0, keepdims=True)
    square[...] = jnp.broadcast_to(sums, square.shape)
    upright = projected.T
    scopies = []
    for dz in range(1, PLANES):
        copy = pltpu.make_async_remote_copy(
            src_ref=square, dst_ref=squares.at[me.plane], send_sem=ssend.at[dz],
            recv_sem=srecv.at[me.plane], device_id=me.other_plane(dz), device_id_type=MESH,
        )
        copy.start()
        scopies.append(copy)
    summed = square[...]
    for dz in range(1, PLANES):
        z = lax.rem(me.plane + dz, PLANES)
        landed(squares.at[z], srecv.at[z])
        summed = summed + squares[z]
    factor = lax.rsqrt(summed * (1.0 / D) + EPS).T[:, 0:1]
    out[...] = (
        stream[...].astype(F32) + upright * factor * post_gain[...].astype(F32)
    ).astype(BF16)
    for copy in zcopies + scopies + [swap]:
        copy.wait_send()
    apart.finish()
    bpart.finish()


VMEM = pl.BlockSpec(memory_space=pltpu.VMEM)
SMEM = pl.BlockSpec(memory_space=pltpu.SMEM)
ANY = pl.BlockSpec(memory_space=pl.ANY)
DMA = pltpu.SemaphoreType.DMA


def params(collective):
    return pltpu.CompilerParams(
        collective_id=collective, has_side_effects=True, vmem_limit_bytes=60 * 1024 * 1024
    )


def per_device(
    residual,
    pre_gain,
    query_weight,
    key_weight,
    value_weight,
    output_weight,
    adapter_down,
    adapter_up_query,
    adapter_up_key,
    adapter_up_value,
    adapter_down_out,
    adapter_up_out,
    post_gain,
    sink_logits,
    prompt_lengths,
    prompt_adapters,
):
    half = residual.shape[0]
    tokens = 2 * half
    own_width = adapter_up_out.shape[1]
    exponent = np.arange(HEAD // 2, dtype=np.float32) * np.float32(2.0 / HEAD)
    freq = np.power(np.float32(10000.0), -exponent).astype(np.float32)
    freq = jnp.asarray(np.concatenate([freq, freq])[None, :])

    exchange = []
    for z in range(PLANES):
        for w in range(2 * CHIPS):
            exchange.append((w * PLANES + z, (4 * z + w % 4) * PLANES + w // 4))
    turned = lax.ppermute(output_weight.T, ("wide", "narrow"), exchange)
    down = jnp.pad(adapter_down, ((0, 0), (0, HEAD - adapter_down.shape[1])))
    stream = lax.dynamic_slice_in_dim(residual, lax.axis_index("narrow") * own_width, own_width, 1)

    shape = jax.ShapeDtypeStruct
    q, k, v = pl.pallas_call(
        project_kernel,
        name="project",
        out_shape=(
            shape((tokens, 2 * HEAD), BF16),
            shape((tokens, HEAD), BF16),
            shape((tokens, HEAD), BF16),
        ),
        in_specs=[SMEM, SMEM, VMEM, VMEM, ANY, ANY, ANY, ANY, VMEM, VMEM, VMEM, VMEM],
        out_specs=(VMEM, VMEM, VMEM),
        scratch_shapes=[
            pltpu.VMEM((half, D), BF16),
            pltpu.VMEM((tokens, D), BF16),
            pltpu.VMEM((CHIPS, 2, ROWS, 256), BF16),
            pltpu.VMEM((CHIPS, 2, ROWS, 256), BF16),
            pltpu.VMEM((CHIPS, 2, ROWS, 128), BF16),
            pltpu.VMEM((tokens, 256), F32),
            pltpu.VMEM((tokens, 256), F32),
            pltpu.VMEM((2, 48, half), F32),
            pltpu.VMEM((48, half), F32),
            pltpu.VMEM((48, half), BF16),
            pltpu.VMEM((PLANES, 2, 48, half), BF16),
            DMA((3, 32)),
            DMA((3, 24)),
            DMA((15,)),
            DMA((PLANES, 2)),
            DMA((5,)),
        ],
        compiler_params=params(0),
    )(
        prompt_lengths, prompt_adapters, residual, pre_gain[None, :], query_weight, key_weight,
        value_weight, down, adapter_up_query, adapter_up_key, adapter_up_value, freq,
    )
    att = pl.pallas_call(
        attend_kernel,
        name="attend",
        out_shape=shape((2 * HEAD + RANK, tokens), BF16),
        in_specs=[SMEM, SMEM, SMEM, VMEM, VMEM, VMEM, VMEM],
        out_specs=VMEM,
        scratch_shapes=[
            pltpu.VMEM((CHIPS, tokens, HEAD), BF16),
            pltpu.VMEM((CHIPS, tokens, HEAD), BF16),
            pltpu.VMEM((2, 1, tokens), F32),
            pltpu.VMEM((2, 1, tokens), F32),
            pltpu.VMEM((2, HEAD, tokens), F32),
            DMA((2, 32)),
            DMA((2, 24)),
            DMA((1,)),
        ],
        compiler_params=params(1),
    )(prompt_lengths, prompt_adapters, sink_logits, q, k, v, adapter_down_out)
    return pl.pallas_call(
        output_kernel,
        name="output",
        out_shape=shape((half, own_width), BF16),
        in_specs=[SMEM, SMEM, VMEM, ANY, VMEM, VMEM, VMEM],
        out_specs=VMEM,
        scratch_shapes=[
            pltpu.VMEM((PLANES, 2 * HEAD + RANK, tokens), BF16),
            pltpu.VMEM((CHIPS, 2, ROWS, HEAD), BF16),
            pltpu.VMEM((CHIPS, 2, ROWS, HEAD), BF16),
            pltpu.VMEM((own_width + RANK, tokens), F32),
            pltpu.VMEM((own_width + RANK, half), BF16),
            pltpu.VMEM((own_width + RANK, half), BF16),
            pltpu.VMEM((8, half), F32),
            pltpu.VMEM((PLANES, 8, half), F32),
            DMA((2, 32)),
            DMA((2, 24)),
            DMA((16,)),
            DMA((20,)),
            DMA((8,)),
            DMA((8,)),
            DMA((3,)),
        ],
        compiler_params=params(2),
    )(
        prompt_lengths, prompt_adapters, att, turned, adapter_up_out, post_gain[None, :], stream
    )


def solution(mesh):
    return jax.shard_map(
        per_device,
        mesh=mesh,
        in_specs=(
            P("wide", None),
            P(),
            P("wide", "narrow"),
            P("wide", "narrow"),
            P("wide", "narrow"),
            P("narrow", "wide"),
            P("wide", "narrow"),
            P(None, "narrow"),
            P(None, "narrow"),
            P(None, "narrow"),
            P("narrow", None),
            P(None, "narrow"),
            P("narrow"),
            P("narrow"),
            P(),
            P(),
        ),
        out_specs=P("wide", "narrow"),
        check_vma=False,
    )
```

```python
import functools

import jax
import jax.numpy as jnp
import numpy as np
from jax import lax
from jax.experimental import pallas as pl
from jax.experimental.pallas import tpu as pltpu
from jax.sharding import PartitionSpec as P

MESH = pl.DeviceIdType.MESH
HEAD = 128
ADAPTERS = 16
RANK = 16
D = 4608
SIDE = 4
CHIPS = 16
PLANES = 8
ROWS = D // (2 * CHIPS)
EPS = 1e-06
SCALE = 0.5
SCORE = 1.0 / 12.0
F32 = jnp.float32
BF16 = jnp.bfloat16


def dot(a, b, ca, cb):
    return lax.dot_general(a, b, (((ca,), (cb,)), ((), ())), preferred_element_type=F32)


class Place:
    def __init__(self):
        wide = lax.axis_index("wide")
        self.plane = lax.axis_index("narrow")
        self.core = lax.rem(wide, 2)
        self.chip = wide // 2
        self.x = self.chip // SIDE
        self.y = lax.rem(self.chip, SIDE)
        self.wide = wide

    def chip_at(self, dx, dy):
        return lax.rem(self.x + dx, SIDE) * SIDE + lax.rem(self.y + dy, SIDE)

    def dev(self, dx, dy, core):
        return (self.chip_at(dx, dy) * 2 + core, self.plane)

    def other_plane(self, dz, core=None):
        core = self.core if core is None else core
        return (self.chip * 2 + core, lax.rem(self.plane + dz, PLANES))


def plane_peers(me):
    peers = [me.dev(0, 0, 1 - me.core)]
    for dx, dy in ((1, 0), (3, 0), (0, 1), (0, 3)):
        peers += [me.dev(dx, dy, 0), me.dev(dx, dy, 1)]
    return peers


def landed(ref, sem):
    pltpu.make_async_copy(ref, ref, sem).wait()


class Part:
    def __init__(self, me, order, unit, send, recv):
        self.me, self.order, self.unit, self.send, self.recv = me, order, unit, send, recv
        self.sent = []

    def rel(self, f, g):
        return (f, g) if self.order == "xy" else (g, f)

    def at(self, f, g):
        return self.unit(self.me.chip_at(*self.rel(f, g)))

    def target(self, f, g, core):
        return self.me.dev(*self.rel(f, g), core)

    def push(self, src, dst, sem, device):
        copy = pltpu.make_async_remote_copy(
            src_ref=src,
            dst_ref=dst,
            send_sem=self.send.at[len(self.sent)],
            recv_sem=sem,
            device_id=device,
            device_id_type=MESH,
        )
        copy.start()
        self.sent.append(copy)

    def label(self, f, g):
        return self.recv.at[f * 4 + g]

    def single(self, f, s):
        return self.recv.at[16 + f * 2 + s]

    def start_pairs(self, pieces):
        me = self.me
        mine = self.unit(me.chip)
        for d in (1, 3):
            for core in (me.core, 1 - me.core):
                for src, sub in pieces(core):
                    self.push(src, sub(mine, me.core), self.single(4 - d, me.core), self.target(d, 0, core))
        for src, sub in pieces(1 - me.core):
            self.push(src, sub(mine, me.core), self.single(0, me.core), self.target(0, 0, 1 - me.core))
        for n, (src, sub) in enumerate(pieces(me.core)):
            pltpu.make_async_copy(src, sub(mine, me.core), self.single(0, me.core)).start()

    def start_own(self, src, dst):
        self.own = src
        for d in (1, 3):
            self.push(src, dst, self.label(4 - d, 0), self.target(d, 0, self.me.core))

    def far(self):
        return 3 - 2 * self.me.core, 1 + 2 * self.me.core

    def spread(self, f, src=None):
        unit = self.at(f, 0)
        for d in (1, 3):
            self.push(unit if src is None else src, unit, self.label(f, 4 - d), self.target(0, d, self.me.core))

    def second_pairs(self):
        landed(self.at(0, 0).at[0], self.single(0, 0))
        landed(self.at(0, 0).at[1], self.single(0, 1))
        self.spread(0)
        for f in (1, 3):
            for s in (0, 1):
                landed(self.at(f, 0).at[s], self.single(f, s))
        self.after_first()

    def second_own(self):
        self.spread(0, self.own)
        self.second_rest()

    def second_rest(self):
        for f in (1, 3):
            landed(self.at(f, 0), self.label(f, 0))
        self.after_first()

    def after_first(self):
        source, step = self.far()
        unit = self.at(source, 0)
        self.push(unit, unit, self.label(2, 0), self.target(step, 0, self.me.core))
        for f in (1, 3):
            self.spread(f)

    def third(self):
        landed(self.at(2, 0), self.label(2, 0))
        self.spread(2)

    def fourth(self, fs=(0, 1, 3, 2)):
        source, step = self.far()
        for f in fs:
            for g in (1, 3):
                landed(self.at(f, g), self.label(f, g))
            unit = self.at(f, source)
            self.push(unit, unit, self.label(f, 2), self.target(0, step, self.me.core))

    def last(self, f):
        landed(self.at(f, 2), self.label(f, 2))

    def finish(self):
        for copy in self.sent:
            copy.wait_send()


def token_facts(lengths, places, adapters=None):
    start = jnp.zeros_like(places)
    adapter = jnp.zeros_like(places)
    begin = jnp.int32(0)
    for p in range(4):
        end = begin + lengths[p]
        member = jnp.logical_and(places >= begin, places < end)
        start = jnp.where(member, begin, start)
        if adapters is not None:
            adapter = jnp.where(member, adapters[p], adapter)
        begin = end
    return start, adapter


def choose(codes, adapter):
    tokens = codes.shape[1]
    spread = jnp.broadcast_to(codes[None], (ADAPTERS, RANK, tokens)).reshape(ADAPTERS * RANK, tokens)
    row = lax.broadcasted_iota(jnp.int32, (ADAPTERS * RANK, tokens), 0) // RANK
    return jnp.where(row == adapter, spread, 0.0).astype(BF16)


def layer_kernel(
    lengths, adapters, sinks, residual, gain, qw, kw, vw, dn, wo, upq, upk, upv, dn_out, up_out, post_gain, freq,
    out,
    raw, normed, wk, wv, wq0, wq1, down, acc, mixed, mixed_in, code_send, codes, code_half,
    query, key, value, kbuf, vbuf, top, total, head_acc, att,
    ring, wo_in, woa, wob, out_acc, swap_send, swap_in, square, squares, stream,
    send, recv, csend, crecv, zsend, zrecv, ssend, srecv, one,
):
    me = Place()
    c = me.core
    half = residual.shape[0]
    tokens = 2 * half
    partner = me.dev(0, 0, 1 - c)
    trade_wide = 4 * me.plane + lax.rem(me.wide, 4)
    trade_plane = me.wide // 4
    foreign = trade_plane != me.plane

    own_rows = pltpu.make_async_copy(residual, raw.at[c], one.at[0])
    own_rows.start()
    own_down = pltpu.make_async_copy(dn, down.at[me.chip, c], one.at[1])
    barrier = pltpu.get_barrier_semaphore()
    peers = plane_peers(me) + [me.other_plane(dz) for dz in range(1, PLANES)]
    for peer in peers:
        pl.semaphore_signal(barrier, inc=1, device_id=peer, device_id_type=MESH)

    @pl.when(foreign)
    def _():
        pl.semaphore_signal(barrier, inc=1, device_id=(trade_wide, trade_plane), device_id_type=MESH)

    for j in range(CHIPS):
        down[j, 1 - c] = jnp.zeros(down.shape[2:], BF16)
    pl.semaphore_wait(barrier, len(peers) + foreign.astype(jnp.int32))

    def part(n, order, buf):
        return Part(me, order, lambda j: buf.at[j], send.at[n], recv.at[n])

    dpart = Part(me, "xy", lambda j: down.at[j, c], send.at[0], recv.at[0])
    kpart, vpart = part(1, "xy", wk), part(2, "yx", wv)
    q0part, q1part = part(3, "xy", wq0), part(4, "yx", wq1)
    keys, values = part(5, "xy", kbuf), part(6, "yx", vbuf)
    apart, bpart = part(7, "xy", woa), part(8, "yx", wob)

    def pieces(source, width, offset):
        def of(core):
            cols = pl.ds(pl.multiple_of(core * width + offset, HEAD), HEAD)
            return [(source.at[:, cols], lambda unit, s: unit.at[s])]

        return of

    def local(src, dst, sem):
        copy = pltpu.make_async_copy(src, dst, sem)
        copy.start()
        return copy

    def remote(src, dst, sems, device):
        copy = pltpu.make_async_remote_copy(
            src_ref=src, dst_ref=dst, send_sem=sems[0], recv_sem=sems[1],
            device_id=device, device_id_type=MESH,
        )
        copy.start()
        return copy

    dpart.start_own(dn, down.at[me.chip, c])
    own_down.start()
    swap_rows = remote(residual, raw.at[c], (one.at[2], one.at[3]), partner)
    kpart.start_pairs(pieces(kw, HEAD, 0))
    vpart.start_pairs(pieces(vw, HEAD, 0))
    q0part.start_pairs(pieces(qw, 2 * HEAD, 0))
    q1part.start_pairs(pieces(qw, 2 * HEAD, HEAD))

    gain_row = gain[...].astype(F32).reshape(1, D)

    def norm(side, begin, end):
        def body(i, carry):
            rows = pl.ds(pl.multiple_of(i * 32, 32), 32)
            source = raw[side, rows, :].astype(F32)
            factor = lax.rsqrt(jnp.mean(source * source, axis=1, keepdims=True) + EPS)
            target = pl.ds(pl.multiple_of(side * half + i * 32, 32), 32)
            normed[target, :] = (source * factor * gain_row).astype(BF16)
            return carry

        lax.fori_loop(begin, end, body, 0)

    own_rows.wait()
    norm(c, 0, half // 32)
    dpart.second_own()
    kpart.second_pairs()
    vpart.second_pairs()
    for p in (dpart, kpart, vpart):
        p.third()
    for p in (dpart, kpart, vpart):
        p.fourth((0, 1, 3))
    q0part.second_pairs()
    q1part.second_pairs()
    for p in (dpart, kpart, vpart):
        p.fourth((2,))
    swap_rows.wait_recv()
    norm(1 - c, 0, half // 64)
    q0part.third()
    q1part.third()
    norm(1 - c, half // 64, half // 32)

    first = me.chip * tokens
    places = first + lax.broadcasted_iota(jnp.int32, (1, tokens), 1)
    start_row, adapter = token_facts(lengths, places, adapters)
    for f in (0, 1, 3, 2):
        dpart.last(f)
    own_down.wait()
    part_codes = dot(normed[...], down[...].reshape(D, 96), 1, 0).T
    kept = jnp.where(adapter == 2 * me.plane, part_codes[0:48], 0.0) + jnp.where(
        adapter == 2 * me.plane + 1, part_codes[48:96], 0.0
    )
    mixed[0] = kept[:, :half]
    mixed[1] = kept[:, half:]
    for p in (q0part, q1part):
        p.fourth((0, 1, 3))
    trade = remote(mixed.at[1 - c], mixed_in, (one.at[4], one.at[5]), partner)

    token = first + lax.broadcasted_iota(jnp.int32, (tokens, HEAD), 0)
    start, unused = token_facts(lengths, token)
    angle = (token - start).astype(F32) * freq[...]
    cosine = jnp.cos(angle)
    sine = jnp.sin(angle)
    sine = jnp.where(lax.broadcasted_iota(jnp.int32, (tokens, HEAD), 1) < HEAD // 2, -sine, sine)

    trade.wait_recv()
    code_send[...] = (mixed[c] + mixed_in[...]).astype(BF16)
    for p in (q0part, q1part):
        p.fourth((2,))
    code_copies = []
    for dz in (4, 3, 5, 2, 6, 1, 7):
        code_copies.append(
            remote(code_send, codes.at[me.plane], (csend.at[dz], crecv.at[me.plane]), me.other_plane(dz))
        )
    wo_copy = pltpu.make_async_remote_copy(
        src_ref=wo, dst_ref=wo_in, send_sem=one.at[6], recv_sem=one.at[7],
        device_id=(trade_wide, trade_plane), device_id_type=MESH,
    )

    @pl.when(foreign)
    def _():
        wo_copy.start()

    @pl.when(jnp.logical_not(foreign))
    def _():
        pltpu.make_async_copy(wo, wo_in, one.at[7]).start()

    def multiply(left, right, o):
        x = lax.rem(me.x + o, SIDE)
        cols = pl.ds(pl.multiple_of(x * (D // SIDE), 128), D // SIDE)
        rows = pl.ds(x * SIDE, SIDE)
        weight = jnp.concatenate(
            [left[rows].reshape(D // SIDE, HEAD), right[rows].reshape(D // SIDE, HEAD)], axis=1
        )
        result = dot(normed[:, cols], weight, 1, 0)
        if o == 0:
            acc[...] = result
        else:
            acc[...] += result

    for f in (0, 1, 3, 2):
        kpart.last(f)
        vpart.last(f)
    for o in (0, 1, 3, 2):
        multiply(wk, wv, o)

    whole = code_send[...].astype(F32)
    for dz in (1, 7, 2, 6, 3, 5, 4):
        z = lax.rem(me.plane + dz, PLANES)
        landed(codes.at[z], crecv.at[z])
        whole = whole + codes[z].astype(F32)
    code_half[c] = whole.astype(BF16)
    trade_codes = remote(code_half.at[c], code_half.at[c], (one.at[8], one.at[9]), partner)
    trade_codes.wait_recv()
    whole = jnp.concatenate([code_half[0], code_half[1]], axis=1).astype(F32)

    def low_rank(slot, up, width):
        chosen = choose(whole[slot * RANK:(slot + 1) * RANK], adapter)
        cols = pl.ds(pl.multiple_of(c * width, width), width)
        return SCALE * dot(chosen, up[:, cols], 0, 0)

    def rotate(x):
        return x * cosine + pltpu.roll(x, HEAD // 2, 1) * sine

    key[...] = rotate(acc[:, :HEAD] + low_rank(1, upk, HEAD)).astype(BF16)
    value[...] = (acc[:, HEAD:] + low_rank(2, upv, HEAD)).astype(BF16)
    for h in (0, 1):
        top[h] = jnp.full((1, tokens), sinks[2 * c + h], F32)
        total[h] = jnp.ones((1, tokens), F32)
        head_acc[h] = jnp.zeros((HEAD, tokens), F32)
    keys.start_own(key, kbuf.at[me.chip])
    values.start_own(value, vbuf.at[me.chip])
    keys.spread(0, key)
    values.spread(0, value)

    for f in (0, 1, 3, 2):
        q0part.last(f)
        q1part.last(f)
    for o in (0, 1, 3, 2):
        multiply(wq0, wq1, o)
    full = acc[...] + low_rank(0, upq, 2 * HEAD)
    query[:, :HEAD] = rotate(full[:, :HEAD]).astype(BF16)
    query[:, HEAD:] = rotate(full[:, HEAD:]).astype(BF16)
    keys.second_rest()
    values.second_rest()

    def block(k, v, chip, heads):
        at = chip * tokens + lax.broadcasted_iota(jnp.int32, (tokens, tokens), 0)
        allowed = jnp.logical_and(at <= places, at >= start_row)
        for h in heads:
            scores = dot(k, query[:, h * HEAD:(h + 1) * HEAD], 1, 1) * SCORE
            scores = jnp.where(allowed, scores, -1e30)
            old = top[h]
            fresh = jnp.maximum(old, jnp.max(scores, axis=0, keepdims=True))
            weights = jnp.exp(scores - fresh)
            factor = jnp.exp(old - fresh)
            total[h] = total[h] * factor + jnp.sum(weights, axis=0, keepdims=True)
            head_acc[h] = head_acc[h] * factor + dot(v, weights.astype(BF16), 0, 0)
            top[h] = fresh

    def visit(fx, fy, heads):
        chip = me.chip_at(fx, fy)

        @pl.when(jnp.logical_and(chip < me.chip, chip + 8 >= me.chip))
        def _():
            block(kbuf[chip], vbuf[chip], chip, heads)

    block(key[...], value[...], me.chip, (0, 1))
    keys.third()
    values.third()
    keys.fourth()
    values.fourth()
    landed(wo_in, one.at[7])
    apart.start_pairs(pieces(wo_in, 2 * HEAD, 0))
    bpart.start_pairs(pieces(wo_in, 2 * HEAD, HEAD))

    def near(i, carry):
        a, b = i // 3, lax.rem(i, 3)
        visit(a + a // 2, b + b // 2, (0, 1))
        return carry

    lax.fori_loop(1, 9, near, 0)
    for f in (0, 1, 3, 2):
        keys.last(f)
        values.last(f)
    apart.second_pairs()
    bpart.second_pairs()

    subs = (pl.ds(0, 128), pl.ds(128, 144))
    zcopies = []

    def hop(src, slot, side, d, h):
        zcopies.append(
            remote(
                src, ring.at[slot, subs[h]], (zsend.at[len(zcopies)], zrecv.at[side * 10 + d * 2 + h]),
                me.other_plane(1 if side == 0 else PLANES - 1),
            )
        )

    def plane_of(side, d):
        return lax.rem(me.plane + (PLANES - d if side == 0 else d), PLANES)

    def arrive(side, d, h):
        landed(ring.at[plane_of(side, d), subs[h]], zrecv.at[side * 10 + d * 2 + h])

    dn_cols = pl.multiple_of(c * 256, 256)
    row = lax.broadcasted_iota(jnp.int32, (ADAPTERS * RANK, tokens), 0) // RANK
    for h in (0, 1):
        def rest(i, carry):
            a = jnp.maximum(i - 4, 0)
            edge = i < 4
            visit(jnp.where(edge, 2, a + a // 2), jnp.where(edge, i, 2), (h,))
            return carry

        lax.fori_loop(0, 7, rest, 0)
        att[h * HEAD:(h + 1) * HEAD] = (head_acc[h] / total[h]).astype(BF16)
        if h == 1:
            terms = dot(dn_out[pl.ds(dn_cols, 2 * HEAD), :], att[0:2 * HEAD], 0, 0)
            terms = jnp.where(row == adapter, terms, 0.0)
            terms = jnp.sum(terms.reshape(ADAPTERS, RANK, tokens), axis=0)
            att[2 * HEAD:2 * HEAD + RANK] = terms.astype(BF16)
        for side in (0, 1):
            hop(att.at[subs[h]], me.plane, side, 1, h)
    keep = local(att, ring.at[me.plane], one.at[10])

    def pass_on(d):
        for h in (0, 1):
            for side in (0, 1):
                arrive(side, d, h)
                if d < 3 or h == side:
                    slot = plane_of(side, d)
                    hop(ring.at[slot, subs[h]], slot, side, d + 1, h)

    def out_multiply(z, opening=False):
        weight = jnp.concatenate(
            [woa[pl.ds(2 * z, 2)].reshape(576, 128), wob[pl.ds(2 * z, 2)].reshape(576, 128)], axis=1
        )
        result = dot(weight, ring[z, pl.ds(0, 256)], 1, 0)
        if opening:
            out_acc[0:576] = result
        else:
            out_acc[0:576] += result

    apart.third()
    bpart.third()
    pass_on(1)
    apart.fourth()
    bpart.fourth()
    odd = lax.rem(me.plane, 2) * 64
    window = pl.ds(pl.multiple_of(me.plane * 576 - odd, 128), 640)
    stream[...] = raw[c, :, window].astype(F32).T
    post = jnp.broadcast_to(post_gain[...].astype(F32).reshape(1, 576), (half, 576)).T
    pass_on(2)
    for f in (0, 1, 3, 2):
        apart.last(f)
        bpart.last(f)
    keep.wait()
    out_multiply(me.plane, True)
    for d in (1, 2):
        for side in (0, 1):
            out_multiply(plane_of(side, d))
    pass_on(3)
    for side in (0, 1):
        out_multiply(plane_of(side, 3))
    arrive(0, 4, 0)
    arrive(1, 4, 1)
    out_multiply(plane_of(0, 4))

    out_acc[576:592] = jnp.sum(ring[:, pl.ds(256, RANK)].astype(F32), axis=0)
    theirs = pl.ds(pl.multiple_of((1 - c) * half, 256), half)
    mine = pl.ds(pl.multiple_of(c * half, 256), half)
    swap_send[...] = out_acc[:, theirs].astype(BF16)
    own_places = first + c * half + lax.broadcasted_iota(jnp.int32, (1, half), 1)
    unused, own_adapter = token_facts(lengths, own_places, adapters)
    swap = remote(swap_send, swap_in, (one.at[11], one.at[12]), partner)
    swap.wait_recv()
    merged = out_acc[:, mine] + swap_in[...].astype(F32)
    chosen = choose(merged[576:592].astype(BF16).astype(F32), own_adapter)
    projected = merged[0:576] + SCALE * dot(up_out[...], chosen, 1, 0)
    sums = jnp.sum(projected * projected, axis=0, keepdims=True)
    square[...] = jnp.broadcast_to(sums, square.shape)
    scopies = []
    for dz in (4, 3, 5, 2, 6, 1, 7):
        scopies.append(
            remote(square, squares.at[me.plane], (ssend.at[dz], srecv.at[me.plane]), me.other_plane(dz))
        )
    weighted = projected * post
    summed = square[...]
    for dz in range(1, PLANES):
        z = lax.rem(me.plane + dz, PLANES)
        landed(squares.at[z], srecv.at[z])
        summed = summed + squares[z]
    factor = lax.rsqrt(summed[0:1] * (1.0 / D) + EPS)
    out[...] = (stream[pl.ds(pl.multiple_of(odd, 64), 576), :] + weighted * factor).astype(BF16)

    for copy in code_copies + zcopies + scopies + [swap_rows, trade, trade_codes, swap]:
        copy.wait_send()
    for p in (dpart, kpart, vpart, q0part, q1part, keys, values, apart, bpart):
        p.finish()

    @pl.when(foreign)
    def _():
        wo_copy.wait_send()


VMEM = pl.BlockSpec(memory_space=pltpu.VMEM)
SMEM = pl.BlockSpec(memory_space=pltpu.SMEM)
ANY = pl.BlockSpec(memory_space=pl.ANY)
DMA = pltpu.SemaphoreType.DMA


def per_device(
    residual,
    pre_gain,
    query_weight,
    key_weight,
    value_weight,
    output_weight,
    adapter_down,
    adapter_up_query,
    adapter_up_key,
    adapter_up_value,
    adapter_down_out,
    adapter_up_out,
    post_gain,
    sink_logits,
    prompt_lengths,
    prompt_adapters,
):
    half = residual.shape[0]
    tokens = 2 * half
    own_width = adapter_up_out.shape[1]
    exponent = np.arange(HEAD // 2, dtype=np.float32) * np.float32(2.0 / HEAD)
    freq = np.power(np.float32(10000.0), -exponent).astype(np.float32)
    freq = jnp.asarray(np.concatenate([freq, freq])[None, :])
    piece = pltpu.VMEM((CHIPS, 2, ROWS, HEAD), BF16)
    turned = pl.pallas_call(
        layer_kernel,
        name="layer",
        out_shape=jax.ShapeDtypeStruct((own_width, half), BF16),
        in_specs=[SMEM, SMEM, SMEM, ANY, VMEM, ANY, ANY, ANY, ANY, ANY] + [VMEM] * 7,
        out_specs=VMEM,
        scratch_shapes=[
            pltpu.VMEM((2, half, D), BF16),
            pltpu.VMEM((tokens, D), BF16),
            piece,
            piece,
            piece,
            piece,
            pltpu.VMEM((CHIPS, 2, ROWS, 96), BF16),
            pltpu.VMEM((tokens, 256), F32),
            pltpu.VMEM((2, 48, half), F32),
            pltpu.VMEM((48, half), F32),
            pltpu.VMEM((48, half), BF16),
            pltpu.VMEM((PLANES, 48, half), BF16),
            pltpu.VMEM((2, 48, half), BF16),
            pltpu.VMEM((tokens, 2 * HEAD), BF16),
            pltpu.VMEM((tokens, HEAD), BF16),
            pltpu.VMEM((tokens, HEAD), BF16),
            pltpu.VMEM((CHIPS, tokens, HEAD), BF16),
            pltpu.VMEM((CHIPS, tokens, HEAD), BF16),
            pltpu.VMEM((2, 1, tokens), F32),
            pltpu.VMEM((2, 1, tokens), F32),
            pltpu.VMEM((2, HEAD, tokens), F32),
            pltpu.VMEM((2 * HEAD + RANK, tokens), BF16),
            pltpu.VMEM((PLANES, 2 * HEAD + RANK, tokens), BF16),
            pltpu.VMEM((ROWS, 4 * HEAD), BF16),
            piece,
            piece,
            pltpu.VMEM((own_width + RANK, tokens), F32),
            pltpu.VMEM((own_width + RANK, half), BF16),
            pltpu.VMEM((own_width + RANK, half), BF16),
            pltpu.VMEM((8, half), F32),
            pltpu.VMEM((PLANES, 8, half), F32),
            pltpu.VMEM((640, half), F32),
            DMA((9, 20)),
            DMA((9, 24)),
            DMA((8,)),
            DMA((8,)),
            DMA((16,)),
            DMA((20,)),
            DMA((8,)),
            DMA((8,)),
            DMA((13,)),
        ],
        compiler_params=pltpu.CompilerParams(
            collective_id=0, has_side_effects=True, vmem_limit_bytes=60 * 1024 * 1024
        ),
    )(
        prompt_lengths, prompt_adapters, sink_logits, residual, pre_gain, query_weight, key_weight,
        value_weight, adapter_down, output_weight.T, adapter_up_query, adapter_up_key, adapter_up_value,
        adapter_down_out, adapter_up_out.T, post_gain, freq,
    )
    return turned.T


def solution(mesh):
    return jax.shard_map(
        per_device,
        mesh=mesh,
        in_specs=(
            P("wide", None),
            P(),
            P("wide", "narrow"),
            P("wide", "narrow"),
            P("wide", "narrow"),
            P("narrow", "wide"),
            P("wide", "narrow"),
            P(None, "narrow"),
            P(None, "narrow"),
            P(None, "narrow"),
            P("narrow", None),
            P(None, "narrow"),
            P("narrow"),
            P("narrow"),
            P(),
            P(),
        ),
        out_specs=P("wide", "narrow"),
        check_vma=False,
    )
```
